32 devices in a mesh: dp: 4 (over y, core), row: 2 (over x), col: 4 (over z).
Axes of the slice: x: 2, y: 2, z: 4, core: 2. Of those that a mesh axis runs over, the one named last changes fastest.
Arguments:
- x_in: bfloat16 [8192, 1024], P(('dp', 'row', 'col')), may hold values from -6 to 6
- ln1_gain: bfloat16 [2, 1024], P(None, ('dp', 'row')), may hold values from 0.25 to 1.75
- ln1_bias: bfloat16 [2, 1024], P(None, ('dp', 'row')), may hold values from -3 to 3
- w_qkv: bfloat16 [2, 1024, 3072], P(None, ('dp', 'row'), 'col'), may hold values from -0.7 to 0.7
- b_qv: bfloat16 [2, 2048], P(None, 'col'), may hold values from -3 to 3
- w_out: bfloat16 [2, 1024, 1024], P(None, 'col', ('dp', 'row')), may hold values from -0.5 to 0.5
- b_out: bfloat16 [2, 1024], P(None, ('dp', 'row')), may hold values from -3 to 3
- ln2_gain: bfloat16 [2, 1024], P(None, ('dp', 'row')), may hold values from 0.25 to 1.75
- ln2_bias: bfloat16 [2, 1024], P(None, ('dp', 'row')), may hold values from -3 to 3
- w_up: bfloat16 [2, 1024, 4096], P(None, ('dp', 'row'), 'col'), may hold values from -0.1875 to 0.1875
- b_up: bfloat16 [2, 4096], P(None, 'col'), may hold values from -3 to 3
- w_down: bfloat16 [2, 4096, 1024], P(None, 'col', ('dp', 'row')), may hold values from -0.09375 to 0.09375
- b_down: bfloat16 [2, 1024], P(None, ('dp', 'row')), may hold values from -3 to 3
- cotangent: bfloat16 [8192, 1024], P(('dp', 'row', 'col')), may hold values from -6 to 6
Outputs:
- out_stream: bfloat16 [8192, 1024], P(('dp', 'row', 'col'))
- grad_in: float32 [8192, 1024], P(('dp', 'row', 'col'))
- ln1_gain_grad: float32 [2, 1024], P(None, ('dp', 'row'))
- ln1_bias_grad: float32 [2, 1024], P(None, ('dp', 'row'))
- w_qkv_grad: float32 [2, 1024, 3072], P(None, ('dp', 'row'), 'col')
- b_qv_grad: float32 [2, 2048], P(None, 'col')
- w_out_grad: float32 [2, 1024, 1024], P(None, 'col', ('dp', 'row'))
- b_out_grad: float32 [2, 1024], P(None, ('dp', 'row'))
- ln2_gain_grad: float32 [2, 1024], P(None, ('dp', 'row'))
- ln2_bias_grad: float32 [2, 1024], P(None, ('dp', 'row'))
- w_up_grad: float32 [2, 1024, 4096], P(None, ('dp', 'row'), 'col')
- b_up_grad: float32 [2, 4096], P(None, 'col')
- w_down_grad: float32 [2, 4096, 1024], P(None, 'col', ('dp', 'row'))
- b_down_grad: float32 [2, 1024], P(None, ('dp', 'row'))
The draws below stay inside these ranges and needn't reach their ends.
All inputs are finite; a program needn't handle non-finite values.
Results may differ from the reference program's by a relative error of at most 0.04.
Values may be sent and summed in bfloat16 or wider, within the bound.
No kernel may reach another device: no remote copies, remote signals or barrier semaphores. Data moves between devices by JAX's collectives and lax.ppermute only.
A program may use at most 192 MiB of HBM per device.

```python
import math
import jax
import jax.numpy as jnp
from jax import lax

D = 1024
HEADS = 16
HEAD_DIM = 64
FF = 4096
SEQ = 1024
LAYERS = 2
TOKENS = 8192


def draw_w_qkv(key, part):
    base = jnp.clip(jax.random.normal(key, (LAYERS, D, HEADS, 3, HEAD_DIM), jnp.float32), -4.0, 4.0) * D ** (-0.5)
    return base.reshape(LAYERS, D, 3 * D).astype(jnp.bfloat16)


def level_of(key, extent, cuts, low, high):
    factor_of, own = 1.0, jax.random.fold_in(key, 6)
    for axis_at, shards_of in cuts:
        heights = jnp.exp(jax.random.uniform(jax.random.fold_in(own, axis_at), (shards_of,), jnp.float32, low / len(cuts), high / len(cuts)))
        factor_of = factor_of * jnp.repeat(heights, extent[axis_at] // shards_of).reshape([-1 if axis == axis_at else 1 for axis in range(len(extent))])
    return factor_of


def gaussian(rng, extent, scale, bound, pieces=(), held_as=jnp.bfloat16):
    values = scale * jax.random.normal(rng, extent, jnp.float32)
    if pieces:
        values = values * level_of(rng, extent, pieces, -0.22, 0.18)
    return jnp.clip(values, -bound, bound).astype(held_as)


def setup_inputs(seed: int = 0) -> dict:
    keys = jax.random.split(jax.random.key(seed), 15)
    x_in = gaussian(keys[0], (TOKENS, D), 1.0, 6.0, ((0, 32),))
    ln1_gain = jnp.clip(1.0 + 0.15 * jax.random.normal(keys[1], (LAYERS, D), jnp.float32), 0.25, 1.75).astype(jnp.bfloat16)
    ln1_bias = gaussian(keys[2], (LAYERS, D), 0.3, 3.0, ((1, 8),))
    w_qkv = draw_w_qkv(jax.random.fold_in(keys[14], 71), 0)
    b_qv = gaussian(keys[4], (LAYERS, 2 * D), 0.3, 3.0, ((1, 4),))
    w_out = gaussian(keys[5], (LAYERS, D, D), (D // 8) ** -0.5, 0.5, ((1, 4), (2, 8)))
    b_out = gaussian(keys[6], (LAYERS, D), 0.3, 3.0, ((1, 8),))
    ln2_gain = jnp.clip(1.0 + 0.15 * jax.random.normal(keys[7], (LAYERS, D), jnp.float32), 0.25, 1.75).astype(jnp.bfloat16)
    ln2_bias = gaussian(keys[8], (LAYERS, D), 0.3, 3.0, ((1, 8),))
    w_up = gaussian(keys[9], (LAYERS, D, FF), D ** -0.5, 0.1875, ((1, 8), (2, 4)))
    b_up = gaussian(keys[10], (LAYERS, FF), 0.3, 3.0, ((1, 4),))
    w_down = gaussian(keys[11], (LAYERS, FF, D), FF ** -0.5, 0.09375, ((1, 4), (2, 8)))
    b_down = gaussian(keys[12], (LAYERS, D), 0.3, 3.0, ((1, 8),))
    cotangent = gaussian(keys[13], (TOKENS, D), 1.0, 6.0, ((0, 32),))
    return dict(x_in=x_in, ln1_gain=ln1_gain, ln1_bias=ln1_bias, w_qkv=w_qkv, b_qv=b_qv, w_out=w_out, b_out=b_out, ln2_gain=ln2_gain, ln2_bias=ln2_bias, w_up=w_up, b_up=b_up, w_down=w_down, b_down=b_down, cotangent=cotangent)


@jax.custom_vjp
def low(v):
    return lax.optimization_barrier(v.astype(jnp.bfloat16)).astype(jnp.float32)

@jax.custom_vjp
def low_back(v):
    return v

def low_keep(v):
    return (low(v), None)

def low_pass(kept, grad):
    return (grad,)

def back_keep(v):
    return (v, None)

def back_low(kept, grad):
    return (low(grad),)
low.defvjp(low_keep, low_pass)
low_back.defvjp(back_keep, back_low)
epsilon = 1e-05
gelu_scale = 0.7978845608028654
gelu_cube = 0.044715

def matmul_high(left, right):
    return jnp.dot(left, right, precision=lax.Precision.HIGHEST)

def layer_norm(values, gain_vec, offset_vec):
    center = lax.optimization_barrier(jnp.mean(values, axis=-1, keepdims=True))
    centered = values - center
    spread = lax.optimization_barrier(jnp.mean(centered * centered, axis=-1, keepdims=True))
    return centered * lax.rsqrt(spread + epsilon) * gain_vec + offset_vec

def gelu_tanh(pre_act):
    return 0.5 * pre_act * (1.0 + jnp.tanh(gelu_scale * (pre_act + gelu_cube * pre_act * pre_act * pre_act)))

def attend(packed_seq):
    grouped = packed_seq.reshape(SEQ, HEADS, 3, HEAD_DIM)
    queries = grouped[:, :, 0]
    keys_seq = grouped[:, :, 1]
    values_seq = grouped[:, :, 2]
    positions = jnp.arange(SEQ, dtype=jnp.int32)
    offset = (positions[None, :] - positions[:, None]).astype(jnp.float32)
    slopes = jnp.exp2(-8.0 * (jnp.arange(HEADS, dtype=jnp.int32).astype(jnp.float32) + 1.0) / HEADS)
    scores = jnp.einsum('qhd,khd->hqk', queries, keys_seq, precision=lax.Precision.HIGHEST) * HEAD_DIM ** (-0.5)
    scores = scores + slopes[:, None, None] * offset[None]
    scores = jnp.where((positions[None, :] <= positions[:, None])[None], scores, -1e+30)
    scores = low_back(scores)
    peak = lax.optimization_barrier(jnp.max(scores, axis=-1, keepdims=True))
    powers = jnp.exp(scores - peak)
    probs = low(powers / lax.optimization_barrier(jnp.sum(powers, axis=-1, keepdims=True)))
    mixed_rows = jnp.einsum('hqk,khd->qhd', probs, values_seq, precision=lax.Precision.HIGHEST)
    return mixed_rows.reshape(SEQ, HEADS * HEAD_DIM)

def one_layer(stream, layer_params):
    gain_one, bias_one, qkv_w, qv_bias, out_w, out_b, gain_two, bias_two, up_w, up_b, down_w, down_b = layer_params
    normed_one = low(layer_norm(stream, gain_one, bias_one))
    pair = qv_bias.reshape(HEADS, 2, HEAD_DIM)
    merged = jnp.stack([pair[:, 0], jnp.zeros_like(pair[:, 0]), pair[:, 1]], axis=1).reshape(3 * D)
    packed = low(low_back(matmul_high(normed_one, qkv_w) + merged))
    mixed_rows = lax.map(jax.checkpoint(attend), packed.reshape(-1, SEQ, 3 * D)).reshape(-1, D)
    mixed_rows = low(low_back(mixed_rows))
    middle = stream + low_back(matmul_high(mixed_rows, out_w) + out_b)
    normed_two = low(layer_norm(middle, gain_two, bias_two))
    pre_act = low_back(matmul_high(normed_two, up_w) + up_b)
    activated = low(gelu_tanh(pre_act))
    return middle + low_back(matmul_high(activated, down_w) + down_b)

def forward(stream, tables):
    for layer_index in range(LAYERS):
        stream = one_layer(stream, tuple((param_table[layer_index] for param_table in tables)))
    return stream

def reference(x_in, ln1_gain, ln1_bias, w_qkv, b_qv, w_out, b_out, ln2_gain, ln2_bias, w_up, b_up, w_down, b_down, cotangent):
    params = tuple((param_table.astype(jnp.float32) for param_table in (ln1_gain, ln1_bias, w_qkv, b_qv, w_out, b_out, ln2_gain, ln2_bias, w_up, b_up, w_down, b_down)))
    sequences = TOKENS // SEQ
    per_group = math.gcd(sequences, max(1, 4096 // SEQ))
    group_rows = per_group * SEQ
    streams = x_in.astype(jnp.float32).reshape(-1, group_rows, D)
    upstreams = cotangent.astype(jnp.float32).reshape(-1, group_rows, D)

    def accumulate(totals, inputs):
        stream, upstream = inputs
        result, pullback = jax.vjp(forward, stream, params)
        input_grad, table_grads = pullback(upstream)
        return (jax.tree.map(jnp.add, totals, table_grads), (result.astype(jnp.bfloat16), input_grad))
    totals, (results, input_grads) = lax.scan(accumulate, jax.tree.map(jnp.zeros_like, params), (streams, upstreams))
    return (results.reshape(TOKENS, D), input_grads.reshape(TOKENS, D), totals[0], totals[1], totals[2], totals[3], totals[4], totals[5], totals[6], totals[7], totals[8], totals[9], totals[10], totals[11])
```

```python
import functools

import jax
import jax.numpy as jnp
from jax import lax
from jax.experimental import pallas as pl
from jax.experimental.pallas import tpu as pltpu
from jax.sharding import Mesh
from jax.sharding import PartitionSpec as P

HEADS = 16
HEAD_DIM = 64
LAYERS = 2

epsilon = 1e-05
gelu_scale = 0.7978845608028654
gelu_cube = 0.044715
F32 = jnp.float32
BF16 = jnp.bfloat16
SWAP = [(0, 1), (1, 0)]


def attend_kernel(heads, blk, nblk, ids_ref, slope_ref, p_ref, o_ref, lse_ref, k_sc, v_sc):
    q_id = ids_ref[0]
    width = heads * HEAD_DIM
    for j in range(nblk):
        src = pl.ds(pl.multiple_of((j ^ q_id) * blk, blk), blk)
        k_sc[j * blk:(j + 1) * blk, :] = p_ref[src, width:2 * width]
        v_sc[j * blk:(j + 1) * blk, :] = p_ref[src, 2 * width:]
    lanes = lax.broadcasted_iota(jnp.int32, (blk, width), 1) // HEAD_DIM
    row = lax.broadcasted_iota(jnp.int32, (blk, blk), 0)
    col = lax.broadcasted_iota(jnp.int32, (blk, blk), 1)
    lse_lane = lax.broadcasted_iota(jnp.int32, (blk, 128), 1)
    for i in range(nblk):
        dst = pl.ds(pl.multiple_of((i ^ q_id) * blk, blk), blk)
        klen = (i + 1) * blk
        kpos = lax.broadcasted_iota(jnp.int32, (1, klen), 1).astype(F32)
        q = p_ref[dst, 0:width] * BF16(HEAD_DIM ** -0.5)

        def head(h, carry):
            out, lse = carry
            qm = jnp.where(lanes == h, q, BF16(0))
            s = lax.dot_general(qm, k_sc[0:klen, :], (((1,), (1,)), ((), ())),
                                preferred_element_type=F32)
            s = s + kpos * slope_ref[h]
            last = jnp.where(col <= row, s[:, klen - blk:], -1e30)
            s = last if i == 0 else jnp.concatenate([s[:, :klen - blk], last], axis=1)
            peak = jnp.max(s, axis=-1, keepdims=True)
            e = jnp.exp(s - peak)
            total = jnp.sum(e, axis=-1, keepdims=True)
            mixed = jnp.dot(e.astype(BF16), v_sc[0:klen, :], preferred_element_type=F32)
            mixed = mixed * (1.0 / total)
            return (jnp.where(lanes == h, mixed, out),
                    jnp.where(lse_lane == h, peak + jnp.log(total), lse))

        out, lse = lax.fori_loop(0, heads, head, (jnp.zeros((blk, width), F32), jnp.zeros((blk, 128), F32)))
        o_ref[dst, :] = out.astype(BF16)
        lse_ref[:, i * blk:(i + 1) * blk] = lse.T[0:8, :]


def attend(packed, ids, slopes, nblk):
    rows, width3 = packed.shape
    width = width3 // 3
    heads = width // HEAD_DIM
    blk = rows // nblk
    return pl.pallas_call(
        functools.partial(attend_kernel, heads, blk, nblk),
        out_shape=(jax.ShapeDtypeStruct((rows, width), BF16), jax.ShapeDtypeStruct((8, rows), F32)),
        in_specs=[pl.BlockSpec(memory_space=pltpu.SMEM), pl.BlockSpec(memory_space=pltpu.SMEM), pl.BlockSpec(memory_space=pltpu.VMEM)],
        out_specs=(pl.BlockSpec(memory_space=pltpu.VMEM), pl.BlockSpec(memory_space=pltpu.VMEM)),
        scratch_shapes=[pltpu.VMEM((rows, width), BF16)] * 2,
        cost_estimate=pl.CostEstimate(flops=12_000_000_000, transcendentals=heads * rows * rows // 2, bytes_accessed=rows * width * 8),
        name="attend",
    )(ids, slopes, packed)


def attend_back_kernel(heads, blk, nblk, ids_ref, slope_ref, p_ref, o_ref, lse_ref, g_ref, out_ref, q_sc, k_sc, v_sc, g_sc, d_sc, dq_sc, dk_sc, dv_sc):
    q_id = ids_ref[0]
    width = heads * HEAD_DIM
    rows = nblk * blk
    pick = (lax.broadcasted_iota(jnp.int32, (8, width), 1) // HEAD_DIM == lax.broadcasted_iota(jnp.int32, (8, width), 0))
    pick = jnp.where(pick, 1.0, 0.0).astype(BF16)
    nt = (((1,), (1,)), ((), ()))
    tn = (((0,), (0,)), ((), ()))
    for j in range(nblk):
        src = pl.ds(pl.multiple_of((j ^ q_id) * blk, blk), blk)
        here = slice(j * blk, (j + 1) * blk)
        q_sc[here, :] = p_ref[src, 0:width] * BF16(HEAD_DIM ** -0.5)
        k_sc[here, :] = p_ref[src, width:2 * width]
        v_sc[here, :] = p_ref[src, 2 * width:]
        g = g_ref[src, :]
        g_sc[here, :] = g
        prod = g.astype(F32) * o_ref[src, :].astype(F32)
        high = prod.astype(BF16)
        rest = (prod - high.astype(F32)).astype(BF16)
        d_sc[:, here] = (lax.dot_general(pick, high, nt, preferred_element_type=F32)
                         + lax.dot_general(pick, rest, nt, preferred_element_type=F32))
    dq_sc[...] = jnp.zeros_like(dq_sc)
    dk_sc[...] = jnp.zeros_like(dk_sc)
    dv_sc[...] = jnp.zeros_like(dv_sc)
    krow = lax.broadcasted_iota(jnp.int32, (blk, blk), 0)
    qcol = lax.broadcasted_iota(jnp.int32, (blk, blk), 1)
    row8 = lax.broadcasted_iota(jnp.int32, (8, rows), 0)

    def head(h, carry):
        slope = slope_ref[h]
        lse_row = jnp.sum(jnp.where(row8 == h, lse_ref[...], 0.0), axis=0, keepdims=True)
        d_row = jnp.sum(jnp.where(row8 == h, d_sc[...], 0.0), axis=0, keepdims=True)
        for j in range(nblk):
            first = j * blk
            n = rows - first
            lane_q = lax.broadcasted_iota(jnp.int32, (n, width), 1) // HEAD_DIM == h
            lane_k = lax.broadcasted_iota(jnp.int32, (blk, width), 1) // HEAD_DIM == h
            qm = jnp.where(lane_q, q_sc[first:, :], BF16(0))
            gm = jnp.where(lane_q, g_sc[first:, :], BF16(0))
            k = k_sc[first:first + blk, :]
            km = jnp.where(lane_k, k, BF16(0))
            s = lax.dot_general(k, qm, nt, preferred_element_type=F32)
            kpos = (lax.broadcasted_iota(jnp.int32, (blk, 1), 0) + first).astype(F32)
            s = (s + kpos * slope) - lse_row[:, first:]
            lead = jnp.where(krow <= qcol, s[:, :blk], -1e30)
            s = lead if n == blk else jnp.concatenate([lead, s[:, blk:]], axis=1)
            p = jnp.exp(s)
            dp = lax.dot_general(v_sc[first:first + blk, :], gm, nt, preferred_element_type=F32)
            ds = (p * (dp - d_row[:, first:])).astype(BF16)
            dv_sc[first:first + blk, :] += jnp.dot(p.astype(BF16), gm, preferred_element_type=F32)
            dk_sc[first:first + blk, :] += jnp.dot(ds, qm, preferred_element_type=F32)
            dq_sc[first:, :] += lax.dot_general(ds, km, tn, preferred_element_type=F32)
        return carry

    lax.fori_loop(0, heads, head, 0)
    for j in range(nblk):
        dst = pl.ds(pl.multiple_of((j ^ q_id) * blk, blk), blk)
        here = slice(j * blk, (j + 1) * blk)
        out_ref[dst, 0:width] = (dq_sc[here, :] * HEAD_DIM ** -0.5).astype(BF16)
        out_ref[dst, width:2 * width] = dk_sc[here, :].astype(BF16)
        out_ref[dst, 2 * width:] = dv_sc[here, :].astype(BF16)


def attend_back(packed, mixed, lse, grad, ids, slopes, nblk):
    rows, width3 = packed.shape
    width = width3 // 3
    heads = width // HEAD_DIM
    blk = rows // nblk
    vm = pl.BlockSpec(memory_space=pltpu.VMEM)
    sm = pl.BlockSpec(memory_space=pltpu.SMEM)
    return pl.pallas_call(
        functools.partial(attend_back_kernel, heads, blk, nblk),
        out_shape=jax.ShapeDtypeStruct((rows, width3), BF16),
        in_specs=[sm, sm, vm, vm, vm, vm],
        out_specs=vm,
        scratch_shapes=[pltpu.VMEM((rows, width), BF16)] * 4 + [pltpu.VMEM((8, rows), F32)] + [pltpu.VMEM((rows, width), F32)] * 3,
        cost_estimate=pl.CostEstimate(flops=24_000_000_000, transcendentals=heads * rows * rows // 2, bytes_accessed=rows * width * 16),
        name="attend_back",
    )(ids, slopes, packed, mixed, lse, grad)


class Paired:
    axes = ("y", "c", "x", "z")
    spec = {"tokens": ("y", "c", "x", "z"), "width": ("y", "c", "x"), "heads": "z"}

    def __init__(self, mesh):
        self.mesh = Mesh(mesh.devices.reshape(-1, 2, mesh.shape["row"], mesh.shape["col"]), self.axes)
        self.places = mesh.shape["col"]

    def move(self, value):
        n = self.places
        pairs = [(a * n + b, b * n + a) for a in range(n) for b in range(n)]
        return lax.ppermute(value, ("c", "x", "z"), pairs)

    def shard(self):
        return lax.axis_index("c") * 2 + lax.axis_index("x")

    def first_block(self):
        return self.shard()

    def enter_width(self, value):
        half = value.shape[-1] // 2
        turned = jnp.concatenate([value[..., half:], value[..., :half]], axis=-1)
        return jnp.where(lax.axis_index("y") == 0, value, turned)

    leave_width = enter_width

    def gather_rows(self, value):
        pair = jnp.concatenate([value, lax.ppermute(value, "x", SWAP)], axis=0)
        return jnp.concatenate([pair, lax.ppermute(pair, "c", SWAP)], axis=0)

    def scatter_rows(self, value):
        half = value.shape[0] // 2
        other = lax.ppermute(value[half:].astype(BF16), "c", SWAP)
        pair = value[:half].astype(F32) + other.astype(F32)
        quarter = half // 2
        other = lax.ppermute(pair[quarter:].astype(BF16), "x", SWAP)
        return pair[:quarter] + other.astype(F32)

    def gather_weight(self, value):
        own = lax.all_gather(value, "z", axis=0, tiled=True)
        return jnp.concatenate([own, lax.ppermute(own, "y", SWAP)], axis=0)

    def scatter_grad(self, value):
        half = value.shape[0] // 2
        other = lax.ppermute(value[half:].astype(BF16), "y", SWAP)
        own = (value[:half] + other.astype(F32)).astype(BF16)
        return lax.psum_scatter(own, "z", scatter_dimension=0, tiled=True)

    def share_slot(self):
        return lax.axis_index("z")

    def width_slot(self):
        return lax.axis_index("y") * 4 + lax.axis_index("c") * 2 + lax.axis_index("x")


class Plain:
    spec = {"tokens": ("dp", "row", "col"), "width": ("dp", "row"), "heads": "col"}
    axes = ("dp", "row", "col")

    def __init__(self, mesh):
        self.mesh = mesh
        self.places = mesh.shape["col"]

    def move(self, value):
        return value

    def shard(self):
        return lax.axis_index("col")

    def first_block(self):
        return jnp.int32(0)

    def enter_width(self, value):
        return value

    leave_width = enter_width

    def gather_rows(self, value):
        return lax.all_gather(value, "col", axis=0, tiled=True)

    def scatter_rows(self, value):
        return lax.psum_scatter(value.astype(BF16), "col", scatter_dimension=0, tiled=True).astype(F32)

    def gather_weight(self, value):
        return lax.all_gather(value, ("dp", "row"), axis=0, tiled=True)

    def scatter_grad(self, value):
        return lax.psum_scatter(value.astype(BF16), ("dp", "row"), scatter_dimension=0, tiled=True)

    def share_slot(self):
        return lax.axis_index("col")

    def width_slot(self):
        return lax.axis_index(("dp", "row"))


def normalize(values):
    center = jnp.mean(values, axis=-1, keepdims=True)
    centered = values - center
    spread = jnp.mean(centered * centered, axis=-1, keepdims=True)
    inverse = lax.rsqrt(spread + epsilon)
    return (centered * inverse, inverse)


def norm_backward(upstream, normal, inverse, gain_vec):
    scaled = upstream * gain_vec
    mean_first = jnp.mean(scaled, axis=-1, keepdims=True)
    second = jnp.mean(scaled * normal, axis=-1, keepdims=True)
    return inverse * (scaled - mean_first - normal * second)


def gelu_parts(pre_act):
    tangent = jnp.tanh(gelu_scale * (pre_act + gelu_cube * pre_act * pre_act * pre_act))
    result = 0.5 * pre_act * (1.0 + tangent)
    derivative = 0.5 * (1.0 + tangent) + 0.5 * pre_act * (1.0 - tangent * tangent) * gelu_scale * (
        1.0 + 3.0 * gelu_cube * pre_act * pre_act
    )
    return (result, derivative)


def dot_nn(left, right):
    return jnp.dot(left, right, preferred_element_type=F32)


def dot_nt(left, right):
    return lax.dot_general(left, right, (((1,), (1,)), ((), ())), preferred_element_type=F32)


def dot_tn(left, right):
    return lax.dot_general(left, right, (((0,), (0,)), ((), ())), preferred_element_type=F32)


def by_kind(weight):
    rows, columns = weight.shape
    return weight.reshape(rows, -1, 3, HEAD_DIM).swapaxes(1, 2).reshape(rows, columns)


def by_head(weight):
    rows, columns = weight.shape
    return weight.reshape(rows, 3, -1, HEAD_DIM).swapaxes(1, 2).reshape(rows, columns)


def local(
    plan,
    x_in,
    ln1_gain,
    ln1_bias,
    w_qkv,
    b_qv,
    w_out,
    b_out,
    ln2_gain,
    ln2_bias,
    w_up,
    b_up,
    w_down,
    b_down,
    cotangent,
):
    places = plan.places
    local_heads = HEADS // places
    width = local_heads * HEAD_DIM
    shard = plan.shard()
    ids = plan.first_block().reshape(1).astype(jnp.int32)
    head_order = (shard * local_heads + jnp.arange(local_heads, dtype=jnp.int32)).astype(F32)
    slopes = jnp.exp2(-8.0 * (head_order + 1.0) / HEADS)

    stream = plan.enter_width(plan.move(x_in)).astype(F32)
    vectors = jnp.concatenate([ln1_gain, ln1_bias, b_out, ln2_gain, ln2_bias, b_down], axis=0)
    head_parts = jnp.concatenate([b_qv, b_up], axis=1)
    small = jnp.concatenate([vectors.reshape(-1), head_parts.reshape(-1)]).reshape(-1, 128)
    small = plan.move(small).reshape(-1)
    vectors = plan.gather_weight(small[: vectors.size].reshape(vectors.shape).T).T.astype(F32)
    head_parts = small[vectors.shape[0] * ln1_gain.shape[1] :].reshape(head_parts.shape).astype(F32)

    blocks = []
    for layer in range(LAYERS):
        attn_w = plan.move(jnp.concatenate([by_kind(w_qkv[layer]), w_out[layer].T], axis=1))
        blocks.append((attn_w, plan.move(w_up[layer]), plan.move(w_down[layer].T)))
    upstream_in = plan.move(cotangent)

    saved = []
    for layer in range(LAYERS):
        gain_one, bias_one, out_bias, gain_two, bias_two, down_bias = [
            vectors[LAYERS * kind + layer][None] for kind in range(6)
        ]
        attn_w, up_w, down_w = [plan.gather_weight(block) for block in blocks[layer]]
        qkv_w, out_w = attn_w[:, : 3 * width], attn_w[:, 3 * width :]
        pair = head_parts[layer, : 2 * width].reshape(local_heads, 2, HEAD_DIM)
        merged = jnp.concatenate(
            [pair[:, 0].reshape(-1), jnp.zeros((width,), F32), pair[:, 1].reshape(-1)]
        )
        up_bias = head_parts[layer, 2 * width :]
        normal_one, inverse_one = normalize(stream)
        rows_one = plan.gather_rows((normal_one * gain_one + bias_one).astype(BF16))
        packed = (dot_nn(rows_one, qkv_w) + merged).astype(BF16)
        mixed, log_totals = attend(packed, ids, slopes, places)
        middle = stream + (plan.scatter_rows(dot_nt(mixed, out_w).astype(BF16)) + out_bias)
        normal_two, inverse_two = normalize(middle)
        rows_two = plan.gather_rows((normal_two * gain_two + bias_two).astype(BF16))
        result, derivative = gelu_parts(dot_nn(rows_two, up_w) + up_bias)
        activated = result.astype(BF16)
        derivative = derivative.astype(BF16)
        stream = middle + (plan.scatter_rows(dot_nt(activated, down_w).astype(BF16)) + down_bias)
        saved.append(
            (
                normal_one,
                inverse_one,
                rows_one,
                packed,
                mixed,
                log_totals,
                normal_two,
                inverse_two,
                rows_two,
                activated,
                derivative,
                qkv_w,
                out_w,
                up_w,
                down_w,
                gain_one,
                gain_two,
            )
        )
    out_stream = plan.move(plan.leave_width(stream.astype(BF16)))

    upstream = plan.enter_width(upstream_in).astype(F32)
    shares = [None] * LAYERS
    vector_sums = [None] * LAYERS
    head_sums = [None] * LAYERS
    for layer in reversed(range(LAYERS)):
        (
            normal_one,
            inverse_one,
            rows_one,
            packed,
            mixed,
            log_totals,
            normal_two,
            inverse_two,
            rows_two,
            activated,
            derivative,
            qkv_w,
            out_w,
            up_w,
            down_w,
            gain_one,
            gain_two,
        ) = saved[layer]
        branch_grad = upstream.astype(BF16)
        down_bias_grad = jnp.sum(branch_grad.astype(F32), axis=0)
        branch_rows = plan.gather_rows(branch_grad)
        pre_grad = (dot_nn(branch_rows, down_w) * derivative.astype(F32)).astype(BF16)
        normed_grad = plan.scatter_rows(dot_nt(pre_grad, up_w).astype(BF16))
        down_grad = plan.scatter_grad(dot_tn(branch_rows, activated).astype(BF16))
        up_grad = plan.scatter_grad(dot_tn(rows_two, pre_grad).astype(BF16))
        up_bias_grad = jnp.sum(pre_grad.astype(F32), axis=0)
        gain_two_grad = jnp.sum(normed_grad * normal_two, axis=0)
        bias_two_grad = jnp.sum(normed_grad, axis=0)
        middle_grad = upstream + norm_backward(normed_grad, normal_two, inverse_two, gain_two)
        attn_grad = middle_grad.astype(BF16)
        out_bias_grad = jnp.sum(attn_grad.astype(F32), axis=0)
        attn_rows = plan.gather_rows(attn_grad)
        mixed_grad = dot_nn(attn_rows, out_w).astype(BF16)
        packed_grad = attend_back(packed, mixed, log_totals, mixed_grad, ids, slopes, places)
        first_grad = plan.scatter_rows(dot_nt(packed_grad, qkv_w).astype(BF16))
        attn_share = plan.scatter_grad(
            jnp.concatenate([dot_tn(rows_one, packed_grad).astype(BF16), dot_tn(attn_rows, mixed).astype(BF16)], axis=1)
        )
        column_sums = jnp.sum(packed_grad.astype(F32), axis=0)
        qv_bias_grad = jnp.concatenate(
            [
                column_sums[:width].reshape(local_heads, 1, HEAD_DIM),
                column_sums[2 * width :].reshape(local_heads, 1, HEAD_DIM),
            ],
            axis=1,
        ).reshape(-1)
        gain_one_grad = jnp.sum(first_grad * normal_one, axis=0)
        bias_one_grad = jnp.sum(first_grad, axis=0)
        upstream = middle_grad + norm_backward(first_grad, normal_one, inverse_one, gain_one)
        vector_sums[layer] = jnp.stack(
            [gain_one_grad, bias_one_grad, out_bias_grad, gain_two_grad, bias_two_grad, down_bias_grad]
        )
        head_sums[layer] = jnp.concatenate([qv_bias_grad, up_bias_grad])
        attn_share = plan.move(attn_share).astype(F32)
        shares[layer] = (
            by_head(attn_share[:, : 3 * width]),
            attn_share[:, 3 * width :].T,
            plan.move(up_grad).astype(F32),
            plan.move(down_grad).astype(F32).T,
        )
    grad_in = plan.move(plan.leave_width(upstream.astype(BF16))).astype(F32)

    vector_rows = plan.leave_width(jnp.stack(vector_sums))
    head_rows = jnp.stack(head_sums)
    slots = jnp.where(
        (jnp.arange(places, dtype=jnp.int32) == shard)[:, None, None], head_rows[None], 0.0
    )
    totals = lax.psum(
        jnp.concatenate([vector_rows.reshape(-1), slots.reshape(-1)]).reshape(-1, 1024), plan.axes
    ).reshape(-1)
    vector_rows = totals[: vector_rows.size].reshape(vector_rows.shape)
    slots = totals[vector_rows.size :].reshape(slots.shape)
    own = ln1_gain.shape[1]
    vector_rows = lax.dynamic_slice_in_dim(vector_rows, plan.width_slot() * own, own, 2)
    head_rows = lax.dynamic_index_in_dim(slots, plan.share_slot(), 0, keepdims=False)

    def stacked(member):
        return jnp.stack([shares[layer][member] for layer in range(LAYERS)])

    return (
        out_stream,
        grad_in,
        vector_rows[:, 0],
        vector_rows[:, 1],
        stacked(0),
        head_rows[:, : 2 * width],
        stacked(1),
        vector_rows[:, 2],
        vector_rows[:, 3],
        vector_rows[:, 4],
        stacked(2),
        head_rows[:, 2 * width :],
        stacked(3),
        vector_rows[:, 5],
    )


def solution(mesh):
    shape = mesh.shape
    paired = shape["dp"] == 4 and shape["row"] == 2 and shape["col"] == 4
    plan = Paired(mesh) if paired else Plain(mesh)
    tokens, wide, heads = plan.spec["tokens"], plan.spec["width"], plan.spec["heads"]
    rows = P(tokens, None)
    vector = P(None, wide)
    inward = P(None, wide, heads)
    outward = P(None, heads, wide)
    per_head = P(None, heads)
    return jax.shard_map(
        functools.partial(local, plan),
        mesh=plan.mesh,
        in_specs=(
            rows, vector, vector, inward, per_head, outward, vector,
            vector, vector, inward, per_head, outward, vector, rows,
        ),
        out_specs=(
            rows, rows, vector, vector, inward, per_head, outward, vector,
            vector, vector, inward, per_head, outward, vector,
        ),
        check_vma=False,
    )
```
